32 devices in a mesh: dom: 8 (over z, y), edge: 4 (over x, core).
Axes of the slice: x: 2, y: 2, z: 4, core: 2. Of those that a mesh axis runs over, the one named last changes fastest.
Arguments:
- src_table: float32 [512, 400], P(('dom', 'edge')), may hold values from -6 to 6
- src_state: float32 [512], P(('dom', 'edge')), may hold values from 0.1 to 30
- dst_table: float32 [512, 400], P(('dom', 'edge')), may hold values from -6 to 6
- dst_state: float32 [512], P(('dom', 'edge')), may hold values from 0.1 to 30
- relations: float32 [4131, 400], replicated, may hold values from -1.5 to 1.5
- edge_src: int32 [2, 16000], P(None, ('dom', 'edge')), may hold values from 0 to 63
- edge_rel: int32 [2, 16000], P(None, ('dom', 'edge')), may hold values from 0 to 4130
- edge_dst: int32 [2, 16000], P(None, ('dom', 'edge')), may hold values from 0 to 63
- negatives: int32 [2, 32, 500], P(None, ('dom', 'edge')), may hold values from 0 to 63
Outputs:
- src_out: float32 [512, 400], P(('dom', 'edge'))
- src_state_out: float32 [512], P(('dom', 'edge'))
- dst_out: float32 [512, 400], P(('dom', 'edge'))
- dst_state_out: float32 [512], P(('dom', 'edge'))
The draws below stay inside these ranges and needn't reach their ends.
All inputs are finite; a program needn't handle non-finite values.
Results may differ from the reference program's by a relative error of at most 0.00013.
Values sent between devices are 32-bit elements; how exact they have to be, the bound alone decides.
No kernel may reach another device: no remote copies, remote signals or barrier semaphores. Data moves between devices by JAX's collectives and lax.ppermute only.
A program may use at most 64 MiB of HBM per device.

```python
import math
import jax
import jax.numpy as jnp
import numpy as np
from jax import lax

D = 400
NREL = 4131
NEG = 500
ENT = 64
NENT = 512
EDGES = 16000
NSPANS = 32
N_DOM = 8


def touch_ends(result, stream_key, least, largest):
    dims = result.shape
    spot = [jax.random.randint(jax.random.fold_in(stream_key, axis), (), 0, dims[axis]) for axis in range(len(dims))]
    result = result.at[tuple(spot)].set(least)
    longest = dims.index(max(dims))
    spot[longest] = (spot[longest] + 1) % dims[longest]
    return result.at[tuple(spot)].set(largest)


def block_scale(stream_key, shape, pieces, smallest, top_value):
    factor_of = 1.0
    for position, parts in pieces:
        heights = jax.random.uniform(jax.random.fold_in(jax.random.fold_in(stream_key, 6), position), (parts,), jnp.float32, smallest / len(pieces), top_value / len(pieces))
        factor_of = factor_of * jnp.repeat(jnp.exp(heights), shape[position] // parts).reshape((-1,) + (1,) * (len(shape) - 1 - position))
    return factor_of


def rank_bounds(amount, slope):
    portions = [(1 << 20) // math.isqrt(standing ** slope) + 1 for standing in range(1, amount + 1)]
    spread = 1 + sum(portions) // (1 << 30)
    return np.cumsum(np.array([max(1, weight // spread) for weight in portions]))


def ranked(own_key, dims, amount, skew):
    listing = rank_bounds(amount, skew)
    lot = jax.random.randint(jax.random.fold_in(own_key, 1), dims, 0, int(listing[amount - 1]))
    grade = jnp.searchsorted(jnp.asarray(listing, jnp.int32), lot, side="right")
    return jax.random.permutation(jax.random.fold_in(own_key, 2), amount)[grade].astype(jnp.int32)


def centred(rng, shape, scale, most, pieces=(), dtype=jnp.bfloat16):
    drawn = jax.random.normal(rng, shape, jnp.float32) * scale
    if len(pieces) > 0:
        drawn = block_scale(rng, shape, pieces, -0.22, 0.18) * drawn
    return jnp.clip(drawn, min=-most, max=most).astype(dtype)


def setup_inputs(seed: int = 0) -> dict:
    splits = jax.random.split(jax.random.key(seed), 10)
    return {
        "src_table": centred(splits[0], (NENT, D), 1.0, 6.0, ((0, 32),), jnp.float32),
        "src_state": jnp.clip(jnp.exp(math.log(30.0) - 5.7037825 * jax.random.uniform(splits[1], (NENT,), jnp.float32) ** block_scale(splits[1], (NENT,), ((0, 32),), -0.2, 0.2)), 0.1, 30.0),
        "dst_table": centred(splits[2], (NENT, D), 1.0, 6.0, ((0, 32),), jnp.float32),
        "dst_state": jnp.clip(jnp.exp(math.log(30.0) - 5.7037825 * jax.random.uniform(splits[3], (NENT,), jnp.float32) ** block_scale(splits[3], (NENT,), ((0, 32),), -0.2, 0.2)), 0.1, 30.0),
        "relations": centred(splits[4], (NREL, D), 0.3, 1.5, (), jnp.float32),
        "edge_src": touch_ends(jax.random.randint(splits[5], (2, EDGES), 0, ENT), jax.random.fold_in(splits[5], 1), 0, ENT - 1).astype(jnp.int32),
        "edge_rel": touch_ends(ranked(splits[6], (2, EDGES), NREL, 2), jax.random.fold_in(splits[6], 3), 0, NREL - 1).astype(jnp.int32),
        "edge_dst": touch_ends(jax.random.randint(splits[7], (2, EDGES), 0, ENT), jax.random.fold_in(splits[7], 1), 0, ENT - 1).astype(jnp.int32),
        "negatives": touch_ends(jax.random.randint(splits[8], (2, NSPANS, NEG), 0, ENT), jax.random.fold_in(splits[8], 1), 0, ENT - 1).astype(jnp.int32),
    }


learn_rate = 0.1
epsilon = 1e-06

def bucket_grads(source_rows, target_rows, relations, src_ids, rel_ids, dst_ids, neg_ids):
    middle = source_rows.shape[1] // 2
    blocks = neg_ids.shape[0]
    source = jnp.take(source_rows, src_ids, axis=0)
    target = jnp.take(target_rows, dst_ids, axis=0)
    relation = jnp.take(relations, rel_ids, axis=0)
    src_real, src_imag = (source[:, :middle], source[:, middle:])
    rel_real, rel_imag = (relation[:, :middle], relation[:, middle:])
    rotated = jnp.concatenate([src_real * rel_real - src_imag * rel_imag, src_real * rel_imag + src_imag * rel_real], axis=1)
    positive = lax.optimization_barrier(jnp.sum(rotated * target, axis=1))
    grouped = rotated.reshape(blocks, -1, rotated.shape[1])
    sampled = jnp.take(target_rows, neg_ids, axis=0)
    negative = jnp.einsum('cen,ckn->cek', grouped, sampled, precision=lax.Precision.HIGHEST)
    pos_weight = -jax.nn.sigmoid(-positive)
    neg_weight = jax.nn.sigmoid(negative)
    from_negs = jnp.einsum('cek,ckn->cen', neg_weight, sampled, precision=lax.Precision.HIGHEST)
    rotated_grad = pos_weight[:, None] * target + from_negs.reshape(rotated.shape)
    sampled_grad = jnp.einsum('cek,cen->ckn', neg_weight, grouped, precision=lax.Precision.HIGHEST)
    grad_real, grad_imag = (rotated_grad[:, :middle], rotated_grad[:, middle:])
    source_grad = jnp.concatenate([grad_real * rel_real + grad_imag * rel_imag, grad_imag * rel_real - grad_real * rel_imag], axis=1)
    src_sum = jnp.zeros_like(source_rows).at[src_ids].add(source_grad)
    dst_sum = jnp.zeros_like(target_rows).at[dst_ids].add(pos_weight[:, None] * rotated)
    dst_sum = dst_sum.at[neg_ids.reshape(-1)].add(sampled_grad.reshape(-1, sampled_grad.shape[2]))
    return (src_sum, dst_sum)

def row_adagrad(table, state, grad):
    state = state + lax.optimization_barrier(jnp.mean(grad * grad, axis=-1))
    table = table - learn_rate * grad / (jnp.sqrt(state)[..., None] + epsilon)
    return (table, state)

def reference(src_table, src_state, dst_table, dst_state, relations, edge_src, edge_rel, edge_dst, negatives):
    groups = N_DOM
    width = src_table.shape[1]
    src_parts = src_table.reshape(groups, -1, width)
    src_sums = src_state.reshape(groups, -1)
    dst_parts = dst_table.reshape(groups, -1, width)
    dst_sums = dst_state.reshape(groups, -1)
    edge_sources = edge_src.reshape(2, groups, -1)
    edge_relations = edge_rel.reshape(2, groups, -1)
    edge_targets = edge_dst.reshape(2, groups, -1)
    neg_groups = negatives.reshape(2, groups, -1, negatives.shape[2])
    for bucket in range(2):
        offset = bucket + 1
        dst_turned = jnp.roll(dst_parts, offset, axis=0)
        sums_turned = jnp.roll(dst_sums, offset, axis=0)

        def one_group(items):
            return bucket_grads(items[0], items[1], relations, items[2], items[3], items[4], items[5])
        src_grad, dst_grad = lax.map(one_group, (src_parts, dst_turned, edge_sources[bucket], edge_relations[bucket], edge_targets[bucket], neg_groups[bucket]))
        src_parts, src_sums = row_adagrad(src_parts, src_sums, src_grad)
        dst_turned, sums_turned = row_adagrad(dst_turned, sums_turned, dst_grad)
        dst_parts = jnp.roll(dst_turned, -offset, axis=0)
        dst_sums = jnp.roll(sums_turned, -offset, axis=0)
    return (src_parts.reshape(-1, width), src_sums.reshape(-1), dst_parts.reshape(-1, width), dst_sums.reshape(-1))
```

```python
import functools

import jax
import jax.numpy as jnp
from jax import lax
from jax.experimental import pallas as pl
from jax.experimental.pallas import tpu as pltpu
from jax.sharding import PartitionSpec as P

learn_rate = 0.1
epsilon = 1e-06
LANES = 128
F32 = jnp.float32
BF16 = jnp.bfloat16
SMEM_SPEC = pl.BlockSpec(memory_space=pltpu.SMEM)


def round_up(value, unit):
    return -(-value // unit) * unit


def half_lanes(width):
    padded = round_up(width // 2 + 1, LANES)
    return width // 2, padded


def lane_ids(shape):
    return lax.broadcasted_iota(jnp.int32, shape, len(shape) - 1)


def row_ids(shape):
    return lax.broadcasted_iota(jnp.int32, shape, len(shape) - 2)


def widened(scratch, value, width):
    half, padded = half_lanes(width)
    scratch[:, :width] = value
    rows = scratch[...]
    lane = lane_ids(rows.shape)
    moved = pltpu.roll(rows, padded - half, 1)
    imag = (lane >= padded) & (lane < padded + half)
    return jnp.where(lane < half, rows, jnp.where(imag, moved, 0.0))


def narrowed(rows, width):
    half, padded = half_lanes(width)
    lane = lane_ids(rows.shape)
    moved = pltpu.roll(rows, 2 * padded - (padded - half), 1)
    return jnp.where(lane < half, rows, moved)[:, :width]


def column_of(row):
    count = row.shape[1]
    square = (count, count)
    return jnp.sum(
        jnp.where(lane_ids(square) == row_ids(square), jnp.broadcast_to(row, square), 0.0),
        axis=1,
        keepdims=True,
    )


def row_of(column):
    count = column.shape[0]
    square = (count, count)
    return jnp.sum(
        jnp.where(lane_ids(square) == row_ids(square), jnp.broadcast_to(column, square), 0.0),
        axis=0,
        keepdims=True,
    )


def state_of(rows, width):
    _, padded = half_lanes(width)
    return jnp.sum(
        jnp.where(lane_ids(rows.shape) == padded - 1, rows, 0.0), axis=1, keepdims=True
    )


def stepped(rows, grad, width):
    _, padded = half_lanes(width)
    state = state_of(rows, width) + jnp.sum(grad * grad, axis=1, keepdims=True) / width
    moved = rows - learn_rate * grad / (jnp.sqrt(state) + epsilon)
    return jnp.where(lane_ids(rows.shape) == padded - 1, state, moved), state


def halves(value):
    high = value.astype(BF16)
    low = (value - high.astype(F32)).astype(BF16)
    return high, low


def thirds(value):
    high = value.astype(BF16)
    rest = value - high.astype(F32)
    middle = rest.astype(BF16)
    return high, middle, (rest - middle.astype(F32)).astype(BF16)


def dot(a, b, dims=((1,), (0,))):
    return lax.dot_general(a, b, (dims, ((), ())), preferred_element_type=F32)


def id_row(scratch, ids):
    scratch[...] = jnp.full(scratch.shape, -1, jnp.int32)
    scratch[:, : ids.shape[1]] = ids
    return scratch[...]


def id_columns(row):
    return jnp.transpose(jnp.broadcast_to(row.astype(F32), (LANES, row.shape[1])))


def one_hot(columns, entities, lanes, used):
    tiles = []
    for start in range(0, lanes, LANES):
        lane = lane_ids(columns.shape) + start
        name = jnp.where(lane < used, lax.rem(lane, entities), -2).astype(F32)
        tiles.append(jnp.where(columns == name, 1.0, 0.0))
    return tiles[0] if len(tiles) == 1 else jnp.concatenate(tiles, axis=1)


def pack_kernel(width, src_ref, src_state_ref, dst_ref, dst_state_ref, out_ref, scratch):
    _, padded = half_lanes(width)
    count = src_ref.shape[0]
    for place, (rows_ref, state_ref) in enumerate(
        ((src_ref, src_state_ref), (dst_ref, dst_state_ref))
    ):
        rows = widened(scratch, rows_ref[...], width)
        lane = lane_ids(rows.shape)
        out_ref[place * count : (place + 1) * count, :] = jnp.where(
            lane == padded - 1, column_of(state_ref[...]), rows
        )


def unpack_kernel(width, rows_ref, out_ref, state_ref):
    rows = rows_ref[...]
    out_ref[...] = narrowed(rows, width)
    state_ref[...] = row_of(state_of(rows, width))


def gather_kernel(width, rel_ids, rel_ref, out_ref, table):
    half, padded = half_lanes(width)
    step = pl.program_id(0)
    chunk = rel_ref.shape[1]
    for start in range(0, chunk, LANES):
        block = rel_ref[:, start : start + LANES]
        real = jnp.transpose(block[:padded])
        real = jnp.where(lane_ids(real.shape) < half, real, 0.0)
        imag = jnp.concatenate([block[half:], jnp.zeros((padded - half, LANES), F32)], axis=0)
        place = pl.ds(pl.multiple_of(step * chunk + start, LANES), LANES)
        table[place, :padded] = real
        table[place, padded:] = jnp.transpose(imag)

    @pl.when(step == pl.num_programs(0) - 1)
    def _():
        edges = rel_ids.shape[1]
        whole = edges // 8 * 8
        for bucket in range(out_ref.shape[0]):
            if whole < out_ref.shape[1]:
                out_ref[bucket, whole:, :] = jnp.zeros((out_ref.shape[1] - whole, out_ref.shape[2]), F32)

            def pick(edge, carry):
                row = rel_ids[bucket, edge]
                out_ref[bucket, pl.ds(edge, 1), :] = table[pl.ds(row, 1), :]
                return carry

            lax.fori_loop(0, edges, pick, 0, unroll=20 if edges % 20 == 0 else 1)


def rotate(table, rel, row, q_ref):
    entities = table.shape[0]
    used = 3 * entities
    lanes = round_up(used, LANES)
    chosen = one_hot(id_columns(row), entities, lanes, used).astype(BF16)
    pieces = list(thirds(table))
    if lanes > used:
        pieces.append(jnp.zeros((lanes - used, table.shape[1]), BF16))
    rows = dot(chosen, jnp.concatenate(pieces, axis=0))
    padded = table.shape[1] // 2
    rel_re, rel_im = rel[:, :padded], rel[:, padded:]
    src_re, src_im = rows[:, :padded], rows[:, padded:]
    q_ref[:, :padded] = src_re * rel_re - src_im * rel_im
    q_ref[:, padded:] = src_re * rel_im + src_im * rel_re


def first_rotate_kernel(shards, packed_ref, rel_ref, src_ids, src_ref, q_ref, ids):
    count = packed_ref.shape[0] // (2 * shards)
    table = jnp.concatenate(
        [packed_ref[2 * k * count : (2 * k + 1) * count, :] for k in range(shards)], axis=0
    )
    src_ref[...] = table
    rotate(table, rel_ref[0], id_row(ids, src_ids[0:1, :]), q_ref)


def next_rotate_kernel(width, grads_ref, table_ref, rel_ref, src_ids, src_ref, q_ref, ids, scratch):
    grad = widened(scratch, jnp.sum(grads_ref[...], axis=0), width)
    table, _ = stepped(table_ref[...], grad, width)
    src_ref[...] = table
    rotate(table, rel_ref[0], id_row(ids, src_ids[1:2, :]), q_ref)


def grads_kernel(width, bucket, shards, packed, split, table_ref, q_ref, r_ref, src_ids, dst_ids, neg_ids, *refs):
    if packed:
        dst_out, grad_ref, ids = refs
        count = table_ref.shape[0] // (2 * shards)
        table = jnp.concatenate(
            [table_ref[(2 * k + 1) * count : (2 * k + 2) * count, :] for k in range(shards)], axis=0
        )
        dst_out[...] = table
    else:
        grad_ref, ids = refs
        table = table_ref[...]
    entities = table.shape[0]
    _, padded = half_lanes(width)
    lanes = round_up(entities, LANES)
    copies = lanes // entities
    edges = q_ref.shape[0]

    high, low = halves(table)
    fill = [jnp.zeros((lanes - copies * entities, table.shape[1]), BF16)] if lanes > copies * entities else []
    both = jnp.concatenate([high] * copies + fill + [low] * copies + fill, axis=0)
    q_high, q_low = halves(q_ref[...])
    scores = dot(q_high, both, ((1,), (1,))) + dot(q_low, both, ((1,), (1,)))
    scores = scores[:, :lanes] + scores[:, lanes:]

    neg_row = id_row(ids, neg_ids[...])
    spot = row_ids((lanes, neg_row.shape[1]))
    name = jnp.where(spot < copies * entities, lax.rem(spot, entities), -2)
    hits = jnp.where(name == neg_row, 1.0, 0.0)
    folded = sum(hits[:, k : k + LANES] for k in range(0, hits.shape[1], LANES))
    counts = jnp.sum(jnp.transpose(folded), axis=0, keepdims=True)

    columns = id_columns(id_row(ids, dst_ids[bucket : bucket + 1, :]))
    hit = one_hot(columns, entities, lanes, copies * entities)
    small = jnp.exp(-jnp.abs(scores))
    part = 1.0 / (1.0 + small)
    rest = small * part
    upper = jnp.where(scores >= 0, part, rest)
    under = jnp.where(scores >= 0, rest, part)
    weight = counts * upper - hit * under

    w_high, w_low = halves(weight)
    if copies >= 2:
        spare = [jnp.zeros((lanes - 2 * entities, table.shape[1]), BF16)] if lanes > 2 * entities else []
        left = jnp.concatenate([w_high, w_low], axis=1)
        right = jnp.concatenate(([high, low] + spare) * 2, axis=0)
    else:
        left = jnp.concatenate([w_high, w_high, w_low], axis=1)
        right = jnp.concatenate([high] + fill + [low] + fill + [high] + fill, axis=0)
    q_grad = dot(left, right)

    turned = jnp.transpose(weight)[:entities, :]
    t_high, t_low = halves(turned)
    tall = dot(jnp.concatenate([t_high, t_low], axis=0), q_high)
    dst_sum = tall[:entities] + tall[entities:] + dot(t_high, q_low)

    rel_re, rel_im = r_ref[0, :, :padded], r_ref[0, :, padded:]
    grad_re, grad_im = q_grad[:, :padded], q_grad[:, padded:]
    src_grad = jnp.concatenate(
        [grad_re * rel_re + grad_im * rel_im, grad_im * rel_re - grad_re * rel_im], axis=1
    )
    src_row = id_row(ids, src_ids[bucket : bucket + 1, :])
    pick = jnp.where(row_ids((entities, edges)) == src_row, 1.0, 0.0).astype(BF16)
    g_high, g_low = halves(src_grad)
    src_sum = dot(pick, g_high) + dot(pick, g_low)
    if split:
        count = entities // shards
        for k in range(shards):
            grad_ref[k, :count, :] = src_sum[k * count : (k + 1) * count]
            grad_ref[k, count:, :] = dst_sum[k * count : (k + 1) * count]
    else:
        grad_ref[:entities, :] = narrowed(src_sum, width)
        grad_ref[entities:, :] = narrowed(dst_sum, width)


def step_kernel(width, grads_ref, table_ref, out_ref, scratch):
    grad = widened(scratch, jnp.sum(grads_ref[...], axis=0), width)
    out_ref[...], _ = stepped(table_ref[...], grad, width)


def finish_kernel(width, grads_ref, src_ref, dst_ref, src_out, src_state_out, dst_out):
    grad = jnp.sum(grads_ref[...], axis=0)
    count = src_ref.shape[0]
    rows, state = stepped(src_ref[...], grad[:count], width)
    src_out[...] = narrowed(rows, width)
    src_state_out[...] = row_of(state)
    dst_out[...], _ = stepped(dst_ref[...], grad[count:], width)


def passed_along(value, axis, steps):
    count = lax.axis_size(axis)
    pairs = [(source, (source + steps) % count) for source in range(count)]
    return lax.ppermute(value, axis, pairs)


def call(kernel, name, out_shape, in_specs, out_specs, scratch=(), prefetch=0, grid=(1,), flops=0, moved=0, vmem=24):
    return pl.pallas_call(
        kernel,
        out_shape=out_shape,
        grid_spec=pltpu.PrefetchScalarGridSpec(
            num_scalar_prefetch=prefetch,
            grid=grid,
            in_specs=in_specs,
            out_specs=out_specs,
            scratch_shapes=list(scratch),
        ),
        compiler_params=pltpu.CompilerParams(vmem_limit_bytes=vmem << 20),
        cost_estimate=pl.CostEstimate(flops=flops, bytes_accessed=moved, transcendentals=0),
        name=name,
    )


def block(shape, at=None):
    at = (0,) * len(shape) if at is None else at
    return pl.BlockSpec(shape, lambda *_: at)


def on_device(
    src_table, src_state, dst_table, dst_state, relations, edge_src, edge_rel, edge_dst, negatives
):
    width = src_table.shape[1]
    own = src_table.shape[0]
    shards = lax.axis_size("edge")
    entities = own * shards
    edges = edge_src.shape[1]
    span = round_up(edges, LANES)
    _, padded = half_lanes(width)
    wide = 2 * padded
    assert negatives.shape[1] == 1 and negatives.shape[2] <= span

    def rows(count):
        return jax.ShapeDtypeStruct((count, wide), F32)

    id_scratch = pltpu.VMEM((1, span), jnp.int32)
    id_block = block(edge_src.shape)
    neg_block = block((1, negatives.shape[2]))
    table_block = block((entities, wide))
    q_block = block((span, wide))
    grads_cost = dict(flops=2 * span * wide * entities * 18, moved=span * wide * 4 * 2)
    rotate_cost = dict(flops=2 * span * wide * entities * 6, moved=span * wide * 4 * 2)

    packed = call(
        functools.partial(pack_kernel, width),
        "pack",
        rows(2 * own),
        [block((own, width)), block((1, own))] * 2,
        block((2 * own, wide)),
        [pltpu.VMEM((own, wide), F32)],
    )(src_table, src_state.reshape(1, own), dst_table, dst_state.reshape(1, own))
    packed = lax.all_gather(packed, "edge", axis=0, tiled=True)
    arrived = passed_along(packed, "dom", 1)

    chunk = 8 * LANES
    steps = -(-relations.shape[0] // chunk)
    rel_rows = call(
        functools.partial(gather_kernel, width),
        "relations",
        jax.ShapeDtypeStruct((2, span, wide), F32),
        [SMEM_SPEC, pl.BlockSpec((width, chunk), lambda i: (0, i))],
        block((2, span, wide)),
        [pltpu.VMEM((steps * chunk, wide), F32)],
        grid=(steps,),
        moved=relations.size * 4,
        vmem=32,
    )(edge_rel, relations.T)

    src_whole, turned = call(
        functools.partial(first_rotate_kernel, shards),
        "rotate0",
        (rows(entities), rows(span)),
        [block((2 * entities, wide)), block((1, span, wide)), id_block],
        (table_block, q_block),
        [id_scratch],
        **rotate_cost,
    )(packed, rel_rows, edge_src)

    dst_whole, grads = call(
        functools.partial(grads_kernel, width, 0, shards, True, False),
        "grads0",
        (rows(entities), jax.ShapeDtypeStruct((2 * entities, width), F32)),
        [block((2 * entities, wide)), q_block, block((1, span, wide)), id_block, id_block, neg_block],
        (table_block, block((2 * entities, width))),
        [id_scratch],
        **grads_cost,
    )(arrived, turned, rel_rows, edge_src, edge_dst, negatives[0])

    grads = lax.all_gather(grads, "edge", axis=0, tiled=False)
    half_block = (shards, entities, width)
    dst_whole = call(
        functools.partial(step_kernel, width),
        "step",
        rows(entities),
        [block(half_block, (0, 1, 0)), table_block],
        table_block,
        [pltpu.VMEM((entities, wide), F32)],
    )(grads, dst_whole)
    dst_whole = passed_along(dst_whole, "dom", 1)

    src_whole, turned = call(
        functools.partial(next_rotate_kernel, width),
        "rotate1",
        (rows(entities), rows(span)),
        [block(half_block), table_block, block((1, span, wide), (1, 0, 0)), id_block],
        (table_block, q_block),
        [id_scratch, pltpu.VMEM((entities, wide), F32)],
        **rotate_cost,
    )(grads, src_whole, rel_rows, edge_src)

    grads = call(
        functools.partial(grads_kernel, width, 1, shards, False, True),
        "grads1",
        jax.ShapeDtypeStruct((shards, 2 * own, wide), F32),
        [table_block, q_block, block((1, span, wide), (1, 0, 0)), id_block, id_block, neg_block],
        block((shards, 2 * own, wide)),
        [id_scratch],
        **grads_cost,
    )(dst_whole, turned, rel_rows, edge_src, edge_dst, negatives[1])

    grads = lax.all_to_all(grads, "edge", 0, 0)
    place = lax.axis_index("edge").reshape(1).astype(jnp.int32)
    own_block = pl.BlockSpec((own, wide), lambda i, place: (place[0], 0))
    src_out, src_state_out, dst_rows = call(
        lambda place_ref, *refs: finish_kernel(width, *refs),
        "finish",
        (
            jax.ShapeDtypeStruct((own, width), F32),
            jax.ShapeDtypeStruct((1, own), F32),
            rows(own),
        ),
        [block((shards, 2 * own, wide)), own_block, own_block],
        (block((own, width)), block((1, own)), block((own, wide))),
        prefetch=1,
    )(place, grads, src_whole, dst_whole)

    dst_rows = passed_along(dst_rows, "dom", lax.axis_size("dom") - 2)
    dst_out, dst_state_out = call(
        functools.partial(unpack_kernel, width),
        "unpack",
        (jax.ShapeDtypeStruct((own, width), F32), jax.ShapeDtypeStruct((1, own), F32)),
        [block((own, wide))],
        (block((own, width)), block((1, own))),
    )(dst_rows)
    return src_out, src_state_out.reshape(own), dst_out, dst_state_out.reshape(own)


def solution(mesh):
    return jax.shard_map(
        on_device,
        mesh=mesh,
        in_specs=(
            P(("dom", "edge"), None),
            P(("dom", "edge")),
            P(("dom", "edge"), None),
            P(("dom", "edge")),
            P(),
            P(None, ("dom", "edge")),
            P(None, ("dom", "edge")),
            P(None, ("dom", "edge")),
            P(None, ("dom", "edge"), None),
        ),
        out_specs=(
            P(("dom", "edge"), None),
            P(("dom", "edge")),
            P(("dom", "edge"), None),
            P(("dom", "edge")),
        ),
        check_vma=False,
    )
```

```python
import functools

import jax
import jax.numpy as jnp
from jax import lax
from jax.experimental import pallas as pl
from jax.experimental.pallas import tpu as pltpu
from jax.sharding import PartitionSpec as P

learn_rate = 0.1
epsilon = 1e-06
LANES = 128
F32 = jnp.float32
BF16 = jnp.bfloat16
SMEM_SPEC = pl.BlockSpec(memory_space=pltpu.SMEM)


def round_up(value, unit):
    return -(-value // unit) * unit


def half_lanes(width):
    padded = round_up(width // 2 + 1, LANES)
    return width // 2, padded


def lane_ids(shape):
    return lax.broadcasted_iota(jnp.int32, shape, len(shape) - 1)


def row_ids(shape):
    return lax.broadcasted_iota(jnp.int32, shape, len(shape) - 2)


def widened(scratch, value, width):
    half, padded = half_lanes(width)
    scratch[:, :width] = value
    rows = scratch[...]
    lane = lane_ids(rows.shape)
    moved = pltpu.roll(rows, padded - half, 1)
    imag = (lane >= padded) & (lane < padded + half)
    return jnp.where(lane < half, rows, jnp.where(imag, moved, 0.0))


def narrowed(rows, width):
    half, padded = half_lanes(width)
    lane = lane_ids(rows.shape)
    moved = pltpu.roll(rows, 2 * padded - (padded - half), 1)
    return jnp.where(lane < half, rows, moved)[:, :width]


def column_of(row):
    count = row.shape[1]
    square = (count, count)
    return jnp.sum(
        jnp.where(lane_ids(square) == row_ids(square), jnp.broadcast_to(row, square), 0.0),
        axis=1,
        keepdims=True,
    )


def row_of(column):
    count = column.shape[0]
    square = (count, count)
    return jnp.sum(
        jnp.where(lane_ids(square) == row_ids(square), jnp.broadcast_to(column, square), 0.0),
        axis=0,
        keepdims=True,
    )


def state_of(rows, width):
    _, padded = half_lanes(width)
    return jnp.sum(
        jnp.where(lane_ids(rows.shape) == padded - 1, rows, 0.0), axis=1, keepdims=True
    )


def stepped(rows, grad, width):
    _, padded = half_lanes(width)
    state = state_of(rows, width) + jnp.sum(grad * grad, axis=1, keepdims=True) / width
    moved = rows - learn_rate * grad / (jnp.sqrt(state) + epsilon)
    return jnp.where(lane_ids(rows.shape) == padded - 1, state, moved), state


def halves(value):
    high = value.astype(BF16)
    low = (value - high.astype(F32)).astype(BF16)
    return high, low


def thirds(value):
    high = value.astype(BF16)
    rest = value - high.astype(F32)
    middle = rest.astype(BF16)
    return high, middle, (rest - middle.astype(F32)).astype(BF16)


def dot(a, b, dims=((1,), (0,))):
    return lax.dot_general(a, b, (dims, ((), ())), preferred_element_type=F32)


def id_columns(row):
    return jnp.transpose(jnp.broadcast_to(row.astype(F32), (LANES, row.shape[1])))


def one_hot(columns, entities, lanes, used):
    tiles = []
    for start in range(0, lanes, LANES):
        lane = lane_ids(columns.shape) + start
        name = jnp.where(lane < used, lax.rem(lane, entities), -2).astype(F32)
        tiles.append(jnp.where(columns == name, 1.0, 0.0))
    return tiles[0] if len(tiles) == 1 else jnp.concatenate(tiles, axis=1)


def pack_kernel(
    width, src_hbm, src_state_hbm, dst_hbm, dst_state_hbm, edge_src, edge_rel, edge_dst, negatives,
    src_out, dst_out, ids_out, src, src_state, dst, dst_state, srcs, rels, dsts, negs, scratch, sems,
):
    pairs = (
        (src_hbm, src), (src_state_hbm, src_state), (dst_hbm, dst), (dst_state_hbm, dst_state),
        (edge_src, srcs), (edge_rel, rels), (edge_dst, dsts), (negatives, negs),
    )
    copies = [pltpu.make_async_copy(a, b, sems.at[k]) for k, (a, b) in enumerate(pairs)]
    for copy in copies:
        copy.start()
    for copy in copies:
        copy.wait()
    _, padded = half_lanes(width)
    for rows_ref, state_ref, out_ref in ((src, src_state, src_out), (dst, dst_state, dst_out)):
        rows = widened(scratch, rows_ref[...], width)
        lane = lane_ids(rows.shape)
        out_ref[...] = jnp.where(lane == padded - 1, column_of(state_ref[...]), rows)
    edges = srcs.shape[1]
    ids_out[...] = jnp.full(ids_out.shape, -1, jnp.int32)
    ids_out[0:2, :edges] = srcs[...]
    ids_out[2:4, :edges] = rels[...]
    ids_out[4:6, :edges] = dsts[...]
    for bucket in range(2):
        ids_out[6 + bucket : 7 + bucket, : negs.shape[2]] = negs[bucket]


def unpack_kernel(width, rows_ref, out_ref, state_ref):
    rows = rows_ref[...]
    out_ref[...] = narrowed(rows, width)
    state_ref[...] = row_of(state_of(rows, width))


def gather_kernel(width, edges, sets, rel_hbm, *refs):
    id_refs, (out_ref, landed, table, sems) = refs[:sets], refs[sets:]
    half, padded = half_lanes(width)
    tiles = 2 * padded // LANES
    names = rel_hbm.shape[1]
    parts = []
    for base in (0, half):
        for start in range(0, padded, LANES):
            size = max(0, min(LANES, half - start))
            parts.append((base + start, size))
    copies = []
    for tile, (start, size) in enumerate(parts):
        copy = None
        if size:
            copy = pltpu.make_async_copy(
                rel_hbm.at[pl.ds(start, size), :], landed.at[pl.ds(start, size), :], sems.at[tile]
            )
            copy.start()
        copies.append(copy)
    for tile, (start, size) in enumerate(parts):
        if copies[tile] is not None:
            copies[tile].wait()
        for first in range(0, names, LANES):
            count = min(LANES, names - first)
            piece = landed[start : start + size, first : first + count]
            if count < LANES:
                piece = jnp.concatenate([piece, jnp.zeros((size, LANES - count), F32)], axis=1)
            if size < LANES:
                piece = jnp.concatenate([piece, jnp.zeros((LANES - size, LANES), F32)], axis=0)
            table[pl.ds(first * tiles + tile, LANES, stride=tiles), :] = jnp.transpose(piece)
    span = out_ref.shape[0] // (2 * sets * tiles)
    whole = edges // 8 * 8
    for bucket in range(2):
        for k in range(sets):
            base = (bucket * sets + k) * span * tiles
            if whole < span:
                out_ref[base + whole * tiles : base + span * tiles, :] = jnp.zeros(
                    ((span - whole) * tiles, LANES), F32
                )

            def pick(edge, carry):
                row = pl.multiple_of(id_refs[k][2 + bucket, edge] * tiles, tiles)
                place = pl.multiple_of(base + edge * tiles, tiles)
                out_ref[pl.ds(place, tiles), :] = table[pl.ds(row, tiles), :]
                return carry

            lax.fori_loop(0, edges, pick, 0, unroll=20 if edges % 20 == 0 else 1)


def relation_rows(r_ref, start, span, tiles):
    halves_ = []
    for base in (0, tiles // 2):
        halves_.append(
            jnp.concatenate(
                [r_ref[pl.ds(start * tiles + base + k, span, stride=tiles), :] for k in range(tiles // 2)],
                axis=1,
            )
        )
    return halves_


def assembled(place, own, pieces, swapped, out_ref):
    shards = 2 * len(pieces)
    partner = place + 1 - 2 * lax.rem(place, 2)
    for who, refs in ((place, pieces), (partner, swapped)):
        for k, ref in enumerate(refs):
            shard = lax.rem(who - 2 * k + shards, shards)
            out_ref[pl.ds(pl.multiple_of(shard * own, own), own), :] = ref[...]


def rotate(table, bucket, sets, span, r_ref, id_refs, ids, q_ref):
    entities, wide = table.shape
    padded, tiles = wide // 2, wide // LANES
    used = 3 * entities
    lanes = round_up(used, LANES)
    pieces = list(thirds(table))
    if lanes > used:
        pieces.append(jnp.zeros((lanes - used, wide), BF16))
    stacked = jnp.concatenate(pieces, axis=0)
    for k in range(sets):
        ids[pl.ds(k, 1), :] = id_refs[k][bucket : bucket + 1, :]

    def one(k, carry):
        chosen = one_hot(id_columns(ids[pl.ds(k, 1), :]), entities, lanes, used).astype(BF16)
        rows = dot(chosen, stacked)
        start = k * span
        rel_re, rel_im = relation_rows(r_ref, start, span, tiles)
        src_re, src_im = rows[:, :padded], rows[:, padded:]
        place = pl.ds(pl.multiple_of(start, span), span)
        q_ref[place, :padded] = src_re * rel_re - src_im * rel_im
        q_ref[place, padded:] = src_re * rel_im + src_im * rel_re
        return carry

    lax.fori_loop(0, sets, one, 0, unroll=sets <= 2)


def first_rotate_kernel(own, sets, place, *refs):
    pieces, swapped, r_ref = refs[:sets], refs[sets : 2 * sets], refs[2 * sets]
    id_refs, (src_ref, q_ref, ids) = refs[2 * sets + 1 : 3 * sets + 1], refs[3 * sets + 1 :]
    assembled(place[0], own, pieces, swapped, src_ref)
    rotate(src_ref[...], 0, sets, q_ref.shape[0] // sets, r_ref, id_refs, ids, q_ref)


def next_rotate_kernel(width, sets, mine_ref, other_ref, table_ref, r_ref, *refs):
    id_refs, (src_ref, q_ref, ids) = refs[:sets], refs[sets:]
    table, _ = stepped(table_ref[...], mine_ref[...] + other_ref[...], width)
    src_ref[...] = table
    rotate(table, 1, sets, q_ref.shape[0] // sets, r_ref, id_refs, ids, q_ref)


def add_grads(width, bucket, sets, table, q_ref, r_ref, id_refs, ids, src_sum, dst_sum):
    entities, wide = table.shape
    padded, tiles = wide // 2, wide // LANES
    lanes = round_up(entities, LANES)
    copies = lanes // entities
    span = q_ref.shape[0] // sets
    high, low = halves(table)
    fill = [jnp.zeros((lanes - copies * entities, wide), BF16)] if lanes > copies * entities else []
    both = jnp.concatenate([high] * copies + fill + [low] * copies + fill, axis=0)
    if copies >= 2:
        spare = [jnp.zeros((lanes - 2 * entities, wide), BF16)] if lanes > 2 * entities else []
        right = jnp.concatenate(([high, low] + spare) * 2, axis=0)
    else:
        right = jnp.concatenate([high] + fill + [low] + fill + [high] + fill, axis=0)
    for k in range(sets):
        for kind in range(3):
            row = (0, 4, 6)[kind] + bucket
            ids[pl.ds(3 * k + kind, 1), :] = id_refs[k][row : row + 1, :]

    def one(k, carry):
        start = k * span
        place = pl.ds(pl.multiple_of(start, span), span)
        q_high, q_low = halves(q_ref[place, :])
        scores = dot(q_high, both, ((1,), (1,))) + dot(q_low, both, ((1,), (1,)))
        scores = scores[:, :lanes] + scores[:, lanes:]

        neg_row = ids[pl.ds(3 * k + 2, 1), :]
        spot = row_ids((lanes, span))
        name = jnp.where(spot < copies * entities, lax.rem(spot, entities), -2)
        hits = jnp.where(name == neg_row, 1.0, 0.0)
        folded = sum(hits[:, at : at + LANES] for at in range(0, span, LANES))
        counts = jnp.sum(jnp.transpose(folded), axis=0, keepdims=True)

        hit = one_hot(id_columns(ids[pl.ds(3 * k + 1, 1), :]), entities, lanes, copies * entities)
        small = jnp.exp(-jnp.abs(scores))
        part = 1.0 / (1.0 + small)
        rest = small * part
        upper = jnp.where(scores >= 0, part, rest)
        under = jnp.where(scores >= 0, rest, part)
        weight = counts * upper - hit * under

        w_high, w_low = halves(weight)
        if copies >= 2:
            left = jnp.concatenate([w_high, w_low], axis=1)
        else:
            left = jnp.concatenate([w_high, w_high, w_low], axis=1)
        q_grad = dot(left, right)

        turned = jnp.transpose(weight)[:entities, :]
        t_high, t_low = halves(turned)
        tall = dot(jnp.concatenate([t_high, t_low], axis=0), q_high)
        dst_part = tall[:entities] + tall[entities:] + dot(t_high, q_low)

        rel_re, rel_im = relation_rows(r_ref, start, span, tiles)
        grad_re, grad_im = q_grad[:, :padded], q_grad[:, padded:]
        src_grad = jnp.concatenate(
            [grad_re * rel_re + grad_im * rel_im, grad_im * rel_re - grad_re * rel_im], axis=1
        )
        pick = jnp.where(row_ids((entities, span)) == ids[pl.ds(3 * k, 1), :], 1.0, 0.0).astype(BF16)
        g_high, g_low = halves(src_grad)
        src_part = dot(pick, g_high) + dot(pick, g_low)
        first = isinstance(k, int) and k == 0
        src_sum[...] = src_part if first else src_sum[...] + src_part
        dst_sum[...] = dst_part if first else dst_sum[...] + dst_part
        return carry

    if sets <= 2:
        for k in range(sets):
            one(k, 0)
    else:
        src_sum[...] = jnp.zeros(src_sum.shape, F32)
        dst_sum[...] = jnp.zeros(dst_sum.shape, F32)
        lax.fori_loop(0, sets, one, 0)


def first_grads_kernel(width, own, sets, place, *refs):
    pieces, swapped, q_ref, r_ref = refs[:sets], refs[sets : 2 * sets], refs[2 * sets], refs[2 * sets + 1]
    id_refs, (dst_ref, src_sum, dst_sum, ids) = refs[2 * sets + 2 : 3 * sets + 2], refs[3 * sets + 2 :]
    assembled(place[0], own, pieces, swapped, dst_ref)
    add_grads(width, 0, sets, dst_ref[...], q_ref, r_ref, id_refs, ids, src_sum, dst_sum)


def last_grads_kernel(width, own, sets, place, table_ref, q_ref, r_ref, *refs):
    id_refs, (mine_ref, other_ref, ids, src_sum, dst_sum) = refs[:sets], refs[sets:]
    add_grads(width, 1, sets, table_ref[...], q_ref, r_ref, id_refs, ids, src_sum, dst_sum)
    partner = place[0] + 1 - 2 * lax.rem(place[0], 2)
    for who, out_ref in ((place[0], mine_ref), (partner, other_ref)):
        rows = pl.ds(pl.multiple_of(who * own, own), own)
        out_ref[:own, :] = src_sum[rows, :]
        out_ref[own:, :] = dst_sum[rows, :]


def step_kernel(width, mine_ref, other_ref, table_ref, out_ref):
    out_ref[...], _ = stepped(table_ref[...], mine_ref[...] + other_ref[...], width)


def finish_kernel(width, mine_ref, other_ref, src_ref, dst_ref, src_out, src_state_out, dst_out):
    grad = mine_ref[...] + other_ref[...]
    count = src_ref.shape[0]
    rows, state = stepped(src_ref[...], grad[:count], width)
    src_out[...] = narrowed(rows, width)
    src_state_out[...] = row_of(state)
    dst_out[...], _ = stepped(dst_ref[...], grad[count:], width)


def moved(value, dom, edge):
    groups, shards = lax.axis_size("dom"), lax.axis_size("edge")
    pairs = [
        (group * shards + place, (group + dom) % groups * shards + edge(place) % shards)
        for group in range(groups)
        for place in range(shards)
    ]
    return lax.ppermute(value, ("dom", "edge"), pairs)


def call(kernel, name, out_shape, in_specs, out_specs, scratch=(), prefetch=0, grid=(1,), flops=0, moved=0, vmem=24):
    return pl.pallas_call(
        kernel,
        out_shape=out_shape,
        grid_spec=pltpu.PrefetchScalarGridSpec(
            num_scalar_prefetch=prefetch,
            grid=grid,
            in_specs=in_specs,
            out_specs=out_specs,
            scratch_shapes=list(scratch),
        ),
        compiler_params=pltpu.CompilerParams(vmem_limit_bytes=int(vmem * 2**20)),
        cost_estimate=pl.CostEstimate(flops=flops, bytes_accessed=moved, transcendentals=0),
        name=name,
    )


def block(shape, at=None):
    at = (0,) * len(shape) if at is None else at
    return pl.BlockSpec(shape, lambda *_: at)


def on_device(
    src_table, src_state, dst_table, dst_state, relations, edge_src, edge_rel, edge_dst, negatives
):
    width = src_table.shape[1]
    own = src_table.shape[0]
    shards = lax.axis_size("edge")
    sets = shards // 2
    entities = own * shards
    edges = edge_src.shape[1]
    span = round_up(edges, LANES)
    half, padded = half_lanes(width)
    wide = 2 * padded
    tiles = wide // LANES
    assert shards % 2 == 0 and half % 8 == 0
    assert negatives.shape[1] == 1 and negatives.shape[2] <= span

    def rows(count):
        return jax.ShapeDtypeStruct((count, wide), F32)

    own_block = block((own, wide))
    ids_block = block((8, span))
    table_block = block((entities, wide))
    q_block = block((sets * span, wide))

    def rel_block(bucket):
        return block((sets * span * tiles, LANES), (bucket, 0))

    big = 24 if sets <= 2 else 48
    work = sets * span * wide
    grads_cost = dict(flops=2 * work * entities * 18, moved=work * 4 * 2, vmem=big)
    rotate_cost = dict(flops=2 * work * entities * 6, moved=work * 4 * 2, vmem=big)

    inputs = (
        src_table, src_state.reshape(1, own), dst_table, dst_state.reshape(1, own),
        edge_src, edge_rel, edge_dst, negatives,
    )
    src_own, dst_own, ids_own = call(
        functools.partial(pack_kernel, width),
        "pack",
        (rows(own), rows(own), jax.ShapeDtypeStruct((8, span), jnp.int32)),
        [pl.BlockSpec(memory_space=pltpu.HBM)] * 8,
        (own_block, own_block, ids_block),
        [pltpu.VMEM(x.shape, x.dtype) for x in inputs]
        + [pltpu.VMEM((own, wide), F32), pltpu.SemaphoreType.DMA((8,))],
        vmem=63.9,
    )(*inputs)

    all_ids = [ids_own] + [moved(ids_own, 0, lambda e, k=k: e + 2 * k) for k in range(1, sets)]
    dst_here = [moved(dst_own, 1, lambda e, k=k: e + 2 * k) for k in range(sets)]
    src_here = [src_own] + [moved(src_own, 0, lambda e, k=k: e + 2 * k) for k in range(1, sets)]

    def swapped(value):
        return moved(value, 0, lambda e: e ^ 1)

    src_there = [swapped(x) for x in src_here]
    dst_there = [swapped(x) for x in dst_here]
    place = lax.axis_index("edge").reshape(1).astype(jnp.int32)

    names = relations.shape[0]
    rel_rows = call(
        functools.partial(gather_kernel, width, edges, sets),
        "relations",
        jax.ShapeDtypeStruct((2 * sets * span * tiles, LANES), F32),
        [pl.BlockSpec(memory_space=pltpu.HBM)] + [SMEM_SPEC] * sets,
        block((2 * sets * span * tiles, LANES)),
        [
            pltpu.VMEM((width, names), F32),
            pltpu.VMEM((round_up(names, LANES) * tiles, LANES), F32),
            pltpu.SemaphoreType.DMA((tiles,)),
        ],
        moved=names * width * 4,
        flops=names * width * 2048,
        vmem=46,
    )(relations.T, *all_ids)

    src_whole, turned = call(
        functools.partial(first_rotate_kernel, own, sets),
        "rotate0",
        (rows(entities), rows(sets * span)),
        [own_block] * (2 * sets) + [rel_block(0)] + [ids_block] * sets,
        (table_block, q_block),
        [pltpu.VMEM((round_up(sets, 8), span), jnp.int32)],
        prefetch=1,
        **rotate_cost,
    )(place, *src_here, *src_there, rel_rows, *all_ids)

    id_scratch = pltpu.VMEM((round_up(3 * sets, 8), span), jnp.int32)
    dst_whole, src_mine, dst_mine = call(
        functools.partial(first_grads_kernel, width, own, sets),
        "grads0",
        (rows(entities),) * 3,
        [own_block] * (2 * sets) + [q_block, rel_block(0)] + [ids_block] * sets,
        (table_block,) * 3,
        [id_scratch],
        prefetch=1,
        **grads_cost,
    )(place, *dst_here, *dst_there, turned, rel_rows, *all_ids)

    dst_other = swapped(dst_mine)
    src_other = swapped(src_mine)
    dst_whole = call(
        functools.partial(step_kernel, width),
        "step",
        rows(entities),
        [table_block] * 3,
        table_block,
    )(dst_mine, dst_other, dst_whole)
    dst_whole = moved(dst_whole, 1, lambda e: e)

    src_whole, turned = call(
        functools.partial(next_rotate_kernel, width, sets),
        "rotate1",
        (rows(entities), rows(sets * span)),
        [table_block] * 3 + [rel_block(1)] + [ids_block] * sets,
        (table_block, q_block),
        [pltpu.VMEM((round_up(sets, 8), span), jnp.int32)],
        **rotate_cost,
    )(src_mine, src_other, src_whole, rel_rows, *all_ids)

    both_block = block((2 * own, wide))
    mine, other = call(
        functools.partial(last_grads_kernel, width, own, sets),
        "grads1",
        (rows(2 * own),) * 2,
        [table_block, q_block, rel_block(1)] + [ids_block] * sets,
        (both_block,) * 2,
        [id_scratch, pltpu.VMEM((entities, wide), F32), pltpu.VMEM((entities, wide), F32)],
        prefetch=1,
        **grads_cost,
    )(place, dst_whole, turned, rel_rows, *all_ids)

    other = swapped(other)
    part_block = pl.BlockSpec((own, wide), lambda i, place: (place[0], 0))
    src_out, src_state_out, dst_rows = call(
        lambda place_ref, *refs: finish_kernel(width, *refs),
        "finish",
        (
            jax.ShapeDtypeStruct((own, width), F32),
            jax.ShapeDtypeStruct((1, own), F32),
            rows(own),
        ),
        [both_block, both_block, part_block, part_block],
        (block((own, width)), block((1, own)), own_block),
        prefetch=1,
    )(place, mine, other, src_whole, dst_whole)

    dst_rows = moved(dst_rows, -2, lambda e: e)
    dst_out, dst_state_out = call(
        functools.partial(unpack_kernel, width),
        "unpack",
        (jax.ShapeDtypeStruct((own, width), F32), jax.ShapeDtypeStruct((1, own), F32)),
        [own_block],
        (block((own, width)), block((1, own))),
    )(dst_rows)
    return src_out, src_state_out.reshape(own), dst_out, dst_state_out.reshape(own)


def solution(mesh):
    return jax.shard_map(
        on_device,
        mesh=mesh,
        in_specs=(
            P(("dom", "edge"), None),
            P(("dom", "edge")),
            P(("dom", "edge"), None),
            P(("dom", "edge")),
            P(),
            P(None, ("dom", "edge")),
            P(None, ("dom", "edge")),
            P(None, ("dom", "edge")),
            P(None, ("dom", "edge"), None),
        ),
        out_specs=(
            P(("dom", "edge"), None),
            P(("dom", "edge")),
            P(("dom", "edge"), None),
            P(("dom", "edge")),
        ),
        check_vma=False,
    )
```

```python
import functools

import jax
import jax.numpy as jnp
from jax import lax
from jax.experimental import pallas as pl
from jax.experimental.pallas import tpu as pltpu
from jax.sharding import PartitionSpec as P

learn_rate = 0.1
epsilon = 1e-06
LANES = 128
F32 = jnp.float32
BF16 = jnp.bfloat16


def round_up(value, unit):
    return -(-value // unit) * unit


def half_lanes(width):
    padded = round_up(width // 2 + 1, LANES)
    return width // 2, padded


def lane_ids(shape):
    return lax.broadcasted_iota(jnp.int32, shape, len(shape) - 1)


def row_ids(shape):
    return lax.broadcasted_iota(jnp.int32, shape, len(shape) - 2)


def widened(scratch, value, width):
    half, padded = half_lanes(width)
    scratch[:, :width] = value
    rows = scratch[...]
    lane = lane_ids(rows.shape)
    moved = pltpu.roll(rows, padded - half, 1)
    imag = (lane >= padded) & (lane < padded + half)
    return jnp.where(lane < half, rows, jnp.where(imag, moved, 0.0))


def narrowed(rows, width):
    half, padded = half_lanes(width)
    lane = lane_ids(rows.shape)
    moved = pltpu.roll(rows, 2 * padded - (padded - half), 1)
    return jnp.where(lane < half, rows, moved)[:, :width]


def column_of(row):
    count = row.shape[1]
    square = (count, count)
    return jnp.sum(
        jnp.where(lane_ids(square) == row_ids(square), jnp.broadcast_to(row, square), 0.0),
        axis=1,
        keepdims=True,
    )


def row_of(column):
    count = column.shape[0]
    square = (count, count)
    return jnp.sum(
        jnp.where(lane_ids(square) == row_ids(square), jnp.broadcast_to(column, square), 0.0),
        axis=0,
        keepdims=True,
    )


def state_of(rows, width):
    _, padded = half_lanes(width)
    return jnp.sum(
        jnp.where(lane_ids(rows.shape) == padded - 1, rows, 0.0), axis=1, keepdims=True
    )


def stepped(rows, grad, width):
    _, padded = half_lanes(width)
    state = state_of(rows, width) + jnp.sum(grad * grad, axis=1, keepdims=True) / width
    moved = rows - learn_rate * grad / (jnp.sqrt(state) + epsilon)
    return jnp.where(lane_ids(rows.shape) == padded - 1, state, moved), state


def halves(value):
    high = value.astype(BF16)
    low = (value - high.astype(F32)).astype(BF16)
    return high, low


def thirds(value):
    high = value.astype(BF16)
    rest = value - high.astype(F32)
    middle = rest.astype(BF16)
    return high, middle, (rest - middle.astype(F32)).astype(BF16)


def dot(a, b, dims=((1,), (0,))):
    return lax.dot_general(a, b, (dims, ((), ())), preferred_element_type=F32)


def id_columns(row):
    return jnp.transpose(jnp.broadcast_to(row, (LANES, row.shape[1])))


def one_hot(columns, entities, lanes, used):
    tiles = []
    for start in range(0, lanes, LANES):
        lane = lane_ids(columns.shape) + start
        name = jnp.where(lane < used, lax.rem(lane, entities), -2).astype(F32)
        tiles.append(jnp.where(columns == name, 1.0, 0.0))
    return tiles[0] if len(tiles) == 1 else jnp.concatenate(tiles, axis=1)


def pack_kernel(
    width, src_hbm, src_state_hbm, dst_hbm, dst_state_hbm, edge_src, edge_rel, edge_dst, negatives,
    src_out, dst_out, src, src_state, dst, dst_state, srcs, rels, dsts, negs, scratch, sems,
):
    pairs = (
        (src_hbm, src), (src_state_hbm, src_state), (dst_hbm, dst), (dst_state_hbm, dst_state),
        (edge_src, srcs), (edge_rel, rels), (edge_dst, dsts), (negatives, negs),
    )
    copies = [pltpu.make_async_copy(a, b, sems.at[k]) for k, (a, b) in enumerate(pairs)]
    for copy in copies:
        copy.start()
    for copy in copies:
        copy.wait()
    _, padded = half_lanes(width)
    for rows_ref, state_ref, out_ref in ((src, src_state, src_out), (dst, dst_state, dst_out)):
        rows = widened(scratch, rows_ref[...], width)
        lane = lane_ids(rows.shape)
        out_ref[: rows.shape[0], :] = jnp.where(lane == padded - 1, column_of(state_ref[...]), rows)
    own, edges = src.shape[0], srcs.shape[1]
    src_out[own:, :] = jnp.full((src_out.shape[0] - own, src_out.shape[1]), -1.0, F32)
    src_out[own + 2 : own + 4, :] = jnp.zeros((2, src_out.shape[1]), F32)
    src_out[own : own + 2, :edges] = srcs[...].astype(F32)
    src_out[own + 2 : own + 4, :edges] = rels[...].astype(F32)
    src_out[own + 4 : own + 6, :edges] = dsts[...].astype(F32)
    for bucket in range(2):
        src_out[own + 6 + bucket : own + 7 + bucket, : negs.shape[2]] = negs[bucket].astype(F32)


def unpack_kernel(width, rows_ref, out_ref, state_ref):
    rows = rows_ref[...]
    out_ref[...] = narrowed(rows, width)
    state_ref[...] = row_of(state_of(rows, width))


def relations_kernel(width, own, sets, rel_hbm, *refs):
    pieces, (out_ref, table, landed, staged, scalars, sems, sem) = refs[:sets], refs[sets:]
    span = pieces[0].shape[1]
    half, padded = half_lanes(width)
    tiles = 2 * padded // LANES
    names = rel_hbm.shape[1]
    parts = []
    for base in (0, half):
        for start in range(0, padded, LANES):
            parts.append((base + start, max(0, min(LANES, half - start))))
    copies = []
    for tile, (start, size) in enumerate(parts):
        copy = None
        if size:
            copy = pltpu.make_async_copy(
                rel_hbm.at[pl.ds(start, size), :], landed.at[pl.ds(start, size), :], sems.at[tile]
            )
            copy.start()
        copies.append(copy)

    def turned(piece, first, tile):
        size = piece.shape[0]
        if size < LANES:
            piece = jnp.concatenate([piece, jnp.zeros((LANES - size, LANES), F32)], axis=0)
        table[pl.ds(first * tiles + tile, LANES, stride=tiles), :] = jnp.transpose(piece)

    for tile, (start, size) in enumerate(parts):
        if copies[tile] is not None:
            copies[tile].wait()
        full = names // LANES

        def one(at, carry):
            first = pl.multiple_of(at * LANES, LANES)
            turned(landed[start : start + size, pl.ds(first, LANES)], first, tile)
            return carry

        lax.fori_loop(0, full, one, 0, unroll=8 if full % 8 == 0 else 1)
        if full * LANES < names:
            piece = landed[start : start + size, full * LANES : names]
            gap = jnp.zeros((size, LANES - piece.shape[1]), F32)
            turned(jnp.concatenate([piece, gap], axis=1), full * LANES, tile)

    chunks = span // LANES
    for bucket in range(2):
        for k in range(sets):
            line = own + 2 + bucket
            row = (pieces[k][line : line + 1, :] * tiles).astype(jnp.int32)
            for chunk in range(chunks):
                at = (bucket * sets + k) * chunks + chunk
                staged[at : at + 1, :] = row[:, chunk * LANES : (chunk + 1) * LANES]
    copy = pltpu.make_async_copy(staged, scalars, sem)
    copy.start()
    copy.wait()

    def some(chunk, carry):
        for lane in range(LANES):
            place = pl.multiple_of(chunk * (LANES * tiles), LANES * tiles) + lane * tiles
            row = pl.multiple_of(scalars[chunk, lane], tiles)
            out_ref[pl.ds(place, tiles), :] = table[pl.ds(row, tiles), :]
        return carry

    lax.fori_loop(0, 2 * sets * chunks, some, 0)


def relation_rows(r_ref, start, span, tiles):
    halves_ = []
    for base in (0, tiles // 2):
        halves_.append(
            jnp.concatenate(
                [r_ref[pl.ds(start * tiles + base + k, span, stride=tiles), :] for k in range(tiles // 2)],
                axis=1,
            )
        )
    return halves_


def assembled(place, own, pieces, swapped, out_ref):
    shards = 2 * len(pieces)
    partner = place + 1 - 2 * lax.rem(place, 2)
    for who, refs in ((place, pieces), (partner, swapped)):
        for k, ref in enumerate(refs):
            shard = lax.rem(who - 2 * k + shards, shards)
            out_ref[pl.ds(pl.multiple_of(shard * own, own), own), :] = ref[:own, :]


def rotate(table, bucket, sets, span, r_ref, id_rows, ids, q_ref):
    entities, wide = table.shape
    padded, tiles = wide // 2, wide // LANES
    used = 3 * entities
    lanes = round_up(used, LANES)
    pieces = list(thirds(table))
    if lanes > used:
        pieces.append(jnp.zeros((lanes - used, wide), BF16))
    stacked = jnp.concatenate(pieces, axis=0)
    for k in range(sets):
        ids[pl.ds(k, 1), :] = id_rows(k, bucket)

    def one(k, carry):
        chosen = one_hot(id_columns(ids[pl.ds(k, 1), :]), entities, lanes, used).astype(BF16)
        rows = dot(chosen, stacked)
        start = k * span
        rel_re, rel_im = relation_rows(r_ref, start, span, tiles)
        src_re, src_im = rows[:, :padded], rows[:, padded:]
        place = pl.ds(pl.multiple_of(start, span), span)
        q_ref[place, :padded] = src_re * rel_re - src_im * rel_im
        q_ref[place, padded:] = src_re * rel_im + src_im * rel_re
        return carry

    lax.fori_loop(0, sets, one, 0, unroll=sets <= 2)


def reader(refs, own):
    return lambda k, row: refs[k][own + row : own + row + 1, :]


def first_rotate_kernel(own, sets, place, *refs):
    pieces, swapped = refs[:sets], refs[sets : 2 * sets]
    r_ref, src_ref, q_ref, ids = refs[2 * sets :]
    assembled(place[0], own, pieces, swapped, src_ref)
    rotate(src_ref[...], 0, sets, q_ref.shape[0] // sets, r_ref, reader(pieces, own), ids, q_ref)


def next_rotate_kernel(width, own, sets, mine_ref, other_ref, rows_ref, *refs):
    pieces, (r_ref, src_ref, q_ref, ids) = refs[:sets], refs[sets:]
    rows, _ = stepped(rows_ref[...], mine_ref[...] + other_ref[...], width)
    src_ref[...] = rows
    rotate(rows, 1, sets, q_ref.shape[0] // sets, r_ref, reader(pieces, own), ids, q_ref)


def add_grads(bucket, sets, table, q_ref, r_ref, id_rows, ids, src_sum, dst_sum):
    entities, wide = table.shape
    padded, tiles = wide // 2, wide // LANES
    lanes = round_up(entities, LANES)
    copies = lanes // entities
    span = q_ref.shape[0] // sets
    high, low = halves(table)
    fill = [jnp.zeros((lanes - copies * entities, wide), BF16)] if lanes > copies * entities else []
    both = jnp.concatenate([high] * copies + fill + [low] * copies + fill, axis=0)
    if copies >= 2:
        spare = [jnp.zeros((lanes - 2 * entities, wide), BF16)] if lanes > 2 * entities else []
        right = jnp.concatenate(([high, low] + spare) * 2, axis=0)
    else:
        right = jnp.concatenate([high] + fill + [low] + fill + [high] + fill, axis=0)
    for k in range(sets):
        for kind in range(3):
            ids[pl.ds(3 * k + kind, 1), :] = id_rows(k, (0, 4, 6)[kind] + bucket)

    def one(k, carry):
        start = k * span
        place = pl.ds(pl.multiple_of(start, span), span)
        q_high, q_low = halves(q_ref[place, :])
        scores = dot(q_high, both, ((1,), (1,))) + dot(q_low, both, ((1,), (1,)))
        scores = scores[:, :lanes] + scores[:, lanes:]

        neg_row = ids[pl.ds(3 * k + 2, 1), :]
        spot = row_ids((lanes, span))
        name = jnp.where(spot < copies * entities, lax.rem(spot, entities), -2).astype(F32)
        hits = jnp.where(name == neg_row, 1.0, 0.0)
        folded = sum(hits[:, at : at + LANES] for at in range(0, span, LANES))
        counts = jnp.sum(jnp.transpose(folded), axis=0, keepdims=True)

        hit = one_hot(id_columns(ids[pl.ds(3 * k + 1, 1), :]), entities, lanes, copies * entities)
        small = jnp.exp(-jnp.abs(scores))
        part = 1.0 / (1.0 + small)
        rest = small * part
        upper = jnp.where(scores >= 0, part, rest)
        under = jnp.where(scores >= 0, rest, part)
        weight = counts * upper - hit * under

        w_high, w_low = halves(weight)
        if copies >= 2:
            left = jnp.concatenate([w_high, w_low], axis=1)
        else:
            left = jnp.concatenate([w_high, w_high, w_low], axis=1)
        q_grad = dot(left, right)

        turned = jnp.transpose(weight)[:entities, :]
        t_high, t_low = halves(turned)
        tall = dot(jnp.concatenate([t_high, t_low], axis=0), q_high)
        dst_part = tall[:entities] + tall[entities:] + dot(t_high, q_low)

        rel_re, rel_im = relation_rows(r_ref, start, span, tiles)
        grad_re, grad_im = q_grad[:, :padded], q_grad[:, padded:]
        src_grad = jnp.concatenate(
            [grad_re * rel_re + grad_im * rel_im, grad_im * rel_re - grad_re * rel_im], axis=1
        )
        pick = jnp.where(row_ids((entities, span)).astype(F32) == ids[pl.ds(3 * k, 1), :], 1.0, 0.0).astype(BF16)
        g_high, g_low = halves(src_grad)
        src_part = dot(pick, g_high) + dot(pick, g_low)
        first = isinstance(k, int) and k == 0
        src_sum[...] = src_part if first else src_sum[...] + src_part
        dst_sum[...] = dst_part if first else dst_sum[...] + dst_part
        return carry

    if sets <= 2:
        for k in range(sets):
            one(k, 0)
    else:
        src_sum[...] = jnp.zeros(src_sum.shape, F32)
        dst_sum[...] = jnp.zeros(dst_sum.shape, F32)
        lax.fori_loop(0, sets, one, 0)


def first_grads_kernel(own, sets, place, *refs):
    pieces, swapped, q_ref, r_ref = refs[:sets], refs[sets : 2 * sets], refs[2 * sets], refs[2 * sets + 1]
    id_refs, (dst_ref, src_sum, dst_sum, ids) = refs[2 * sets + 2 : 3 * sets + 2], refs[3 * sets + 2 :]
    assembled(place[0], own, pieces, swapped, dst_ref)
    add_grads(0, sets, dst_ref[...], q_ref, r_ref, reader(id_refs, own), ids, src_sum, dst_sum)


def last_grads_kernel(own, sets, place, table_ref, q_ref, r_ref, *refs):
    id_refs, (mine_ref, other_ref, ids, src_sum, dst_sum) = refs[:sets], refs[sets:]
    add_grads(1, sets, table_ref[...], q_ref, r_ref, reader(id_refs, own), ids, src_sum, dst_sum)
    partner = place[0] + 1 - 2 * lax.rem(place[0], 2)
    for who, out_ref in ((place[0], mine_ref), (partner, other_ref)):
        rows = pl.ds(pl.multiple_of(who * own, own), own)
        out_ref[:own, :] = src_sum[rows, :]
        out_ref[own:, :] = dst_sum[rows, :]


def step_kernel(width, mine_ref, other_ref, table_ref, out_ref):
    out_ref[...], _ = stepped(table_ref[...], mine_ref[...] + other_ref[...], width)


def finish_kernel(width, mine_ref, other_ref, src_ref, dst_ref, src_out, src_state_out, dst_out):
    grad = mine_ref[...] + other_ref[...]
    count = src_ref.shape[0]
    rows, state = stepped(src_ref[...], grad[:count], width)
    src_out[...] = narrowed(rows, width)
    src_state_out[...] = row_of(state)
    dst_out[...], _ = stepped(dst_ref[...], grad[count:], width)


def moved(value, dom, edge):
    groups, shards = lax.axis_size("dom"), lax.axis_size("edge")
    pairs = [
        (group * shards + place, (group + dom) % groups * shards + edge(place) % shards)
        for group in range(groups)
        for place in range(shards)
    ]
    return lax.ppermute(value, ("dom", "edge"), pairs)


def call(kernel, name, out_shape, in_specs, out_specs, scratch=(), prefetch=0, grid=(1,), flops=0, moved=0, vmem=24):
    return pl.pallas_call(
        kernel,
        out_shape=out_shape,
        grid_spec=pltpu.PrefetchScalarGridSpec(
            num_scalar_prefetch=prefetch,
            grid=grid,
            in_specs=in_specs,
            out_specs=out_specs,
            scratch_shapes=list(scratch),
        ),
        compiler_params=pltpu.CompilerParams(vmem_limit_bytes=int(vmem * 2**20)),
        cost_estimate=pl.CostEstimate(flops=flops, bytes_accessed=moved, transcendentals=0),
        name=name,
    )


def block(shape, at=None):
    at = (0,) * len(shape) if at is None else at
    return pl.BlockSpec(shape, lambda *_: at)


def on_device(
    src_table, src_state, dst_table, dst_state, relations, edge_src, edge_rel, edge_dst, negatives
):
    width = src_table.shape[1]
    own = src_table.shape[0]
    shards = lax.axis_size("edge")
    sets = shards // 2
    entities = own * shards
    edges = edge_src.shape[1]
    span = round_up(edges, LANES)
    half, padded = half_lanes(width)
    wide = 2 * padded
    tiles = wide // LANES
    assert shards % 2 == 0 and half % 8 == 0 and own % 8 == 0 and span == wide
    assert negatives.shape[1] == 1 and negatives.shape[2] <= span

    def rows(count):
        return jax.ShapeDtypeStruct((count, wide), F32)

    own_block = block((own, wide))
    src_block = block((own + 8, wide))
    table_block = block((entities, wide))
    q_block = block((sets * span, wide))

    def rel_block(bucket):
        return block((sets * span * tiles, LANES), (bucket, 0))

    names = relations.shape[0]
    listed = (round_up(2 * sets * span // LANES, 8), LANES)
    rotate_scratch = [pltpu.VMEM((round_up(sets, 8), span), F32)]
    big = 24 if sets <= 2 else 48
    work = sets * span * wide
    grads_cost = dict(flops=2 * work * entities * 18, moved=work * 4 * 2, vmem=big)
    rotate_cost = dict(flops=2 * work * entities * 6, moved=work * 4 * 2, vmem=big)

    inputs = (
        src_table, src_state.reshape(1, own), dst_table, dst_state.reshape(1, own),
        edge_src, edge_rel, edge_dst, negatives,
    )
    src_own, dst_own = call(
        functools.partial(pack_kernel, width),
        "pack",
        (rows(own + 8), rows(own)),
        [pl.BlockSpec(memory_space=pltpu.HBM)] * 8,
        (src_block, own_block),
        [pltpu.VMEM(x.shape, x.dtype) for x in inputs]
        + [pltpu.VMEM((own, wide), F32), pltpu.SemaphoreType.DMA((8,))],
        vmem=63.9,
    )(*inputs)

    dst_here = [moved(dst_own, 1, lambda e, k=k: e + 2 * k) for k in range(sets)]
    src_here = [src_own] + [moved(src_own, 0, lambda e, k=k: e + 2 * k) for k in range(1, sets)]

    def swapped(value):
        return moved(value, 0, lambda e: e ^ 1)

    src_there = [swapped(x) for x in src_here]
    place = lax.axis_index("edge").reshape(1).astype(jnp.int32)

    rel_shape = (2 * sets * span * tiles, LANES)
    rel_rows = call(
        functools.partial(relations_kernel, width, own, sets),
        "relations",
        jax.ShapeDtypeStruct(rel_shape, F32),
        [pl.BlockSpec(memory_space=pltpu.HBM)] + [src_block] * sets,
        block(rel_shape),
        [
            pltpu.VMEM((round_up(names, LANES) * tiles, LANES), F32),
            pltpu.VMEM((width, names), F32),
            pltpu.VMEM(listed, jnp.int32),
            pltpu.SMEM(listed, jnp.int32),
            pltpu.SemaphoreType.DMA((tiles,)),
            pltpu.SemaphoreType.DMA(()),
        ],
        moved=names * width * 4,
        flops=names * width * 2048,
        vmem=46,
    )(relations.T, *src_here)

    rel_rows, dst_here = lax.optimization_barrier((rel_rows, dst_here))
    dst_there = [swapped(x) for x in dst_here]

    src_whole, turned = call(
        functools.partial(first_rotate_kernel, own, sets),
        "rotate0",
        (rows(entities), rows(sets * span)),
        [src_block] * (2 * sets) + [rel_block(0)],
        (table_block, q_block),
        rotate_scratch,
        prefetch=1,
        **rotate_cost,
    )(place, *src_here, *src_there, rel_rows)

    id_scratch = pltpu.VMEM((round_up(3 * sets, 8), span), F32)
    dst_whole, src_mine, dst_mine = call(
        functools.partial(first_grads_kernel, own, sets),
        "grads0",
        (rows(entities),) * 3,
        [own_block] * (2 * sets) + [q_block, rel_block(0)] + [src_block] * sets,
        (table_block,) * 3,
        [id_scratch],
        prefetch=1,
        **grads_cost,
    )(place, *dst_here, *dst_there, turned, rel_rows, *src_here)

    dst_other = swapped(dst_mine)
    src_other = swapped(src_mine)
    dst_whole = call(
        functools.partial(step_kernel, width),
        "step",
        rows(entities),
        [table_block] * 3,
        table_block,
    )(dst_mine, dst_other, dst_whole)
    dst_whole = moved(dst_whole, 1, lambda e: e)

    src_whole, turned = call(
        functools.partial(next_rotate_kernel, width, own, sets),
        "rotate1",
        (rows(entities), rows(sets * span)),
        [table_block] * 3 + [src_block] * sets + [rel_block(1)],
        (table_block, q_block),
        rotate_scratch,
        **rotate_cost,
    )(src_mine, src_other, src_whole, *src_here, rel_rows)

    both_block = block((2 * own, wide))
    mine, other = call(
        functools.partial(last_grads_kernel, own, sets),
        "grads1",
        (rows(2 * own),) * 2,
        [table_block, q_block, rel_block(1)] + [src_block] * sets,
        (both_block,) * 2,
        [id_scratch, pltpu.VMEM((entities, wide), F32), pltpu.VMEM((entities, wide), F32)],
        prefetch=1,
        **grads_cost,
    )(place, dst_whole, turned, rel_rows, *src_here)

    other = swapped(other)
    part_block = pl.BlockSpec((own, wide), lambda i, place: (place[0], 0))
    src_out, src_state_out, dst_rows = call(
        lambda place_ref, *refs: finish_kernel(width, *refs),
        "finish",
        (
            jax.ShapeDtypeStruct((own, width), F32),
            jax.ShapeDtypeStruct((1, own), F32),
            rows(own),
        ),
        [both_block, both_block, part_block, part_block],
        (block((own, width)), block((1, own)), own_block),
        prefetch=1,
    )(place, mine, other, src_whole, dst_whole)

    dst_rows = moved(dst_rows, -2, lambda e: e)
    dst_out, dst_state_out = call(
        functools.partial(unpack_kernel, width),
        "unpack",
        (jax.ShapeDtypeStruct((own, width), F32), jax.ShapeDtypeStruct((1, own), F32)),
        [own_block],
        (block((own, width)), block((1, own))),
    )(dst_rows)
    return src_out, src_state_out.reshape(own), dst_out, dst_state_out.reshape(own)


def solution(mesh):
    return jax.shard_map(
        on_device,
        mesh=mesh,
        in_specs=(
            P(("dom", "edge"), None),
            P(("dom", "edge")),
            P(("dom", "edge"), None),
            P(("dom", "edge")),
            P(),
            P(None, ("dom", "edge")),
            P(None, ("dom", "edge")),
            P(None, ("dom", "edge")),
            P(None, ("dom", "edge"), None),
        ),
        out_specs=(
            P(("dom", "edge"), None),
            P(("dom", "edge")),
            P(("dom", "edge"), None),
            P(("dom", "edge")),
        ),
        check_vma=False,
    )
```

```python
import functools

import jax
import jax.numpy as jnp
from jax import lax
from jax.experimental import pallas as pl
from jax.experimental.pallas import tpu as pltpu
from jax.sharding import PartitionSpec as P

learn_rate = 0.1
epsilon = 1e-06
LANES = 128
F32 = jnp.float32
BF16 = jnp.bfloat16


def round_up(value, unit):
    return -(-value // unit) * unit


def half_lanes(width):
    padded = round_up(width // 2 + 1, LANES)
    return width // 2, padded


def lane_ids(shape):
    return lax.broadcasted_iota(jnp.int32, shape, len(shape) - 1)


def row_ids(shape):
    return lax.broadcasted_iota(jnp.int32, shape, len(shape) - 2)


def widened(scratch, value, width):
    half, padded = half_lanes(width)
    scratch[:, :width] = value
    rows = scratch[...]
    lane = lane_ids(rows.shape)
    moved = pltpu.roll(rows, padded - half, 1)
    imag = (lane >= padded) & (lane < padded + half)
    return jnp.where(lane < half, rows, jnp.where(imag, moved, 0.0))


def narrowed(rows, width):
    half, padded = half_lanes(width)
    lane = lane_ids(rows.shape)
    moved = pltpu.roll(rows, 2 * padded - (padded - half), 1)
    return jnp.where(lane < half, rows, moved)[:, :width]


def column_of(row):
    count = row.shape[1]
    square = (count, count)
    return jnp.sum(
        jnp.where(lane_ids(square) == row_ids(square), jnp.broadcast_to(row, square), 0.0),
        axis=1,
        keepdims=True,
    )


def row_of(column):
    count = column.shape[0]
    square = (count, count)
    return jnp.sum(
        jnp.where(lane_ids(square) == row_ids(square), jnp.broadcast_to(column, square), 0.0),
        axis=0,
        keepdims=True,
    )


def state_of(rows, width):
    _, padded = half_lanes(width)
    return jnp.sum(
        jnp.where(lane_ids(rows.shape) == padded - 1, rows, 0.0), axis=1, keepdims=True
    )


def stepped(rows, grad, width):
    _, padded = half_lanes(width)
    state = state_of(rows, width) + jnp.sum(grad * grad, axis=1, keepdims=True) / width
    moved = rows - learn_rate * grad / (jnp.sqrt(state) + epsilon)
    return jnp.where(lane_ids(rows.shape) == padded - 1, state, moved), state


def halves(value):
    high = value.astype(BF16)
    low = (value - high.astype(F32)).astype(BF16)
    return high, low


def thirds(value):
    high = value.astype(BF16)
    rest = value - high.astype(F32)
    middle = rest.astype(BF16)
    return high, middle, (rest - middle.astype(F32)).astype(BF16)


def dot(a, b, dims=((1,), (0,))):
    return lax.dot_general(a, b, (dims, ((), ())), preferred_element_type=F32)


def id_columns(row):
    return jnp.transpose(jnp.broadcast_to(row, (LANES, row.shape[1])))


def one_hot(columns, entities, lanes, used):
    tiles = []
    for start in range(0, lanes, LANES):
        lane = lane_ids(columns.shape) + start
        name = jnp.where(lane < used, lax.rem(lane, entities), -2).astype(F32)
        tiles.append(jnp.where(columns == name, 1.0, 0.0))
    return tiles[0] if len(tiles) == 1 else jnp.concatenate(tiles, axis=1)


def pack_kernel(
    width, src_hbm, src_state_hbm, dst_hbm, dst_state_hbm, edge_src, edge_rel, edge_dst, negatives,
    src_out, dst_out, src, src_state, dst, dst_state, srcs, rels, dsts, negs, scratch, sems,
):
    pairs = (
        (src_hbm, src), (src_state_hbm, src_state), (dst_hbm, dst), (dst_state_hbm, dst_state),
        (edge_src, srcs), (edge_rel, rels), (edge_dst, dsts), (negatives, negs),
    )
    copies = [pltpu.make_async_copy(a, b, sems.at[k]) for k, (a, b) in enumerate(pairs)]
    for copy in copies:
        copy.start()
    for copy in copies:
        copy.wait()
    _, padded = half_lanes(width)
    for rows_ref, state_ref, out_ref in ((src, src_state, src_out), (dst, dst_state, dst_out)):
        rows = widened(scratch, rows_ref[...], width)
        lane = lane_ids(rows.shape)
        out_ref[: rows.shape[0], :] = jnp.where(lane == padded - 1, column_of(state_ref[...]), rows)
    own, edges = src.shape[0], srcs.shape[1]
    src_out[own:, :] = jnp.full((src_out.shape[0] - own, src_out.shape[1]), -1.0, F32)
    src_out[own + 2 : own + 4, :] = jnp.zeros((2, src_out.shape[1]), F32)
    src_out[own : own + 2, :edges] = srcs[...].astype(F32)
    src_out[own + 2 : own + 4, :edges] = rels[...].astype(F32)
    src_out[own + 4 : own + 6, :edges] = dsts[...].astype(F32)
    for bucket in range(2):
        src_out[own + 6 + bucket : own + 7 + bucket, : negs.shape[2]] = negs[bucket].astype(F32)


def unpack_kernel(width, rows_ref, out_ref, state_ref):
    rows = rows_ref[...]
    out_ref[...] = narrowed(rows, width)
    state_ref[...] = row_of(state_of(rows, width))


def relations_kernel(width, own, sets, rel_hbm, *refs):
    pieces, (out_ref, table, landed, staged, scalars, sems, sem) = refs[:sets], refs[sets:]
    span = pieces[0].shape[1]
    half, padded = half_lanes(width)
    tiles = 2 * padded // LANES
    names = rel_hbm.shape[1]
    parts = []
    for base in (0, half):
        for start in range(0, padded, LANES):
            parts.append((base + start, max(0, min(LANES, half - start))))
    copies = []
    for tile, (start, size) in enumerate(parts):
        copy = None
        if size:
            copy = pltpu.make_async_copy(
                rel_hbm.at[pl.ds(start, size), :], landed.at[pl.ds(start, size), :], sems.at[tile]
            )
            copy.start()
        copies.append(copy)

    def turned(piece, first, tile):
        size = piece.shape[0]
        if size < LANES:
            piece = jnp.concatenate([piece, jnp.zeros((LANES - size, LANES), F32)], axis=0)
        table[pl.ds(first * tiles + tile, LANES, stride=tiles), :] = jnp.transpose(piece)

    for tile, (start, size) in enumerate(parts):
        if copies[tile] is not None:
            copies[tile].wait()
        full = names // LANES

        def one(at, carry):
            first = pl.multiple_of(at * LANES, LANES)
            turned(landed[start : start + size, pl.ds(first, LANES)], first, tile)
            return carry

        lax.fori_loop(0, full, one, 0, unroll=8 if full % 8 == 0 else 1)
        if full * LANES < names:
            piece = landed[start : start + size, full * LANES : names]
            gap = jnp.zeros((size, LANES - piece.shape[1]), F32)
            turned(jnp.concatenate([piece, gap], axis=1), full * LANES, tile)

    chunks = span // LANES
    for bucket in range(2):
        for k in range(sets):
            line = own + 2 + bucket
            row = (pieces[k][line : line + 1, :] * tiles).astype(jnp.int32)
            for chunk in range(chunks):
                at = (bucket * sets + k) * chunks + chunk
                staged[at : at + 1, :] = row[:, chunk * LANES : (chunk + 1) * LANES]
    copy = pltpu.make_async_copy(staged, scalars, sem)
    copy.start()
    copy.wait()

    def some(chunk, carry):
        for lane in range(LANES):
            place = pl.multiple_of(chunk * (LANES * tiles), LANES * tiles) + lane * tiles
            row = pl.multiple_of(scalars[chunk, lane], tiles)
            out_ref[pl.ds(place, tiles), :] = table[pl.ds(row, tiles), :]
        return carry

    lax.fori_loop(0, 2 * sets * chunks, some, 0)


def relation_rows(r_ref, start, span, tiles):
    halves_ = []
    for base in (0, tiles // 2):
        halves_.append(
            jnp.concatenate(
                [r_ref[pl.ds(start * tiles + base + k, span, stride=tiles), :] for k in range(tiles // 2)],
                axis=1,
            )
        )
    return halves_


def assembled(place, own, pieces, swapped, out_ref):
    shards = 2 * len(pieces)
    partner = place + 1 - 2 * lax.rem(place, 2)
    for who, refs in ((place, pieces), (partner, swapped)):
        for k, ref in enumerate(refs):
            shard = lax.rem(who - 2 * k + shards, shards)
            out_ref[pl.ds(pl.multiple_of(shard * own, own), own), :] = ref[:own, :]


def rotate(table, bucket, sets, span, r_ref, id_rows, ids, q_ref):
    entities, wide = table.shape
    padded, tiles = wide // 2, wide // LANES
    used = 3 * entities
    lanes = round_up(used, LANES)
    pieces = list(thirds(table))
    if lanes > used:
        pieces.append(jnp.zeros((lanes - used, wide), BF16))
    stacked = jnp.concatenate(pieces, axis=0)
    for k in range(sets):
        ids[pl.ds(k, 1), :] = id_rows(k, bucket)

    def one(k, carry):
        chosen = one_hot(id_columns(ids[pl.ds(k, 1), :]), entities, lanes, used).astype(BF16)
        rows = dot(chosen, stacked)
        start = k * span
        rel_re, rel_im = relation_rows(r_ref, start, span, tiles)
        src_re, src_im = rows[:, :padded], rows[:, padded:]
        place = pl.ds(pl.multiple_of(start, span), span)
        q_ref[place, :padded] = src_re * rel_re - src_im * rel_im
        q_ref[place, padded:] = src_re * rel_im + src_im * rel_re
        return carry

    lax.fori_loop(0, sets, one, 0, unroll=sets <= 2)


def reader(refs, own):
    return lambda k, row: refs[k][own + row : own + row + 1, :]


def first_rotate_kernel(own, sets, place, *refs):
    pieces, swapped = refs[:sets], refs[sets : 2 * sets]
    r_ref, src_ref, q_ref, ids = refs[2 * sets :]
    assembled(place[0], own, pieces, swapped, src_ref)
    rotate(src_ref[...], 0, sets, q_ref.shape[0] // sets, r_ref, reader(pieces, own), ids, q_ref)


def next_rotate_kernel(width, own, sets, mine_ref, other_ref, rows_ref, *refs):
    pieces, (r_ref, src_ref, q_ref, ids) = refs[:sets], refs[sets:]
    rows, _ = stepped(rows_ref[...], mine_ref[...] + other_ref[...], width)
    src_ref[...] = rows
    rotate(rows, 1, sets, q_ref.shape[0] // sets, r_ref, reader(pieces, own), ids, q_ref)


def add_grads(bucket, sets, table, q_ref, r_ref, id_rows, ids, src_sum, dst_sum):
    entities, wide = table.shape
    padded, tiles = wide // 2, wide // LANES
    lanes = round_up(entities, LANES)
    copies = lanes // entities
    span = q_ref.shape[0] // sets
    high, low = halves(table)
    fill = [jnp.zeros((lanes - copies * entities, wide), BF16)] if lanes > copies * entities else []
    both = jnp.concatenate([high] * copies + fill + [low] * copies + fill, axis=0)
    if copies >= 2:
        spare = [jnp.zeros((lanes - 2 * entities, wide), BF16)] if lanes > 2 * entities else []
        right = jnp.concatenate(([high, low] + spare) * 2, axis=0)
    else:
        right = jnp.concatenate([high] + fill + [low] + fill + [high] + fill, axis=0)
    for k in range(sets):
        for kind in range(3):
            ids[pl.ds(3 * k + kind, 1), :] = id_rows(k, (0, 4, 6)[kind] + bucket)

    def one(k, carry):
        start = k * span
        place = pl.ds(pl.multiple_of(start, span), span)
        q_high, q_low = halves(q_ref[place, :])
        scores = dot(q_high, both, ((1,), (1,))) + dot(q_low, both, ((1,), (1,)))
        scores = scores[:, :lanes] + scores[:, lanes:]

        neg_row = ids[pl.ds(3 * k + 2, 1), :]
        spot = row_ids((lanes, span))
        name = jnp.where(spot < copies * entities, lax.rem(spot, entities), -2).astype(F32)
        hits = jnp.where(name == neg_row, 1.0, 0.0)
        folded = sum(hits[:, at : at + LANES] for at in range(0, span, LANES))
        counts = jnp.sum(jnp.transpose(folded), axis=0, keepdims=True)

        hit = one_hot(id_columns(ids[pl.ds(3 * k + 1, 1), :]), entities, lanes, copies * entities)
        small = jnp.exp(-jnp.abs(scores))
        part = 1.0 / (1.0 + small)
        rest = small * part
        upper = jnp.where(scores >= 0, part, rest)
        under = jnp.where(scores >= 0, rest, part)
        weight = counts * upper - hit * under

        w_high, w_low = halves(weight)
        if copies >= 2:
            left = jnp.concatenate([w_high, w_low], axis=1)
        else:
            left = jnp.concatenate([w_high, w_high, w_low], axis=1)
        q_grad = dot(left, right)

        turned = jnp.transpose(weight)[:entities, :]
        t_high, t_low = halves(turned)
        tall = dot(jnp.concatenate([t_high, t_low], axis=0), q_high)
        dst_part = tall[:entities] + tall[entities:] + dot(t_high, q_low)

        rel_re, rel_im = relation_rows(r_ref, start, span, tiles)
        grad_re, grad_im = q_grad[:, :padded], q_grad[:, padded:]
        src_grad = jnp.concatenate(
            [grad_re * rel_re + grad_im * rel_im, grad_im * rel_re - grad_re * rel_im], axis=1
        )
        pick = jnp.where(row_ids((entities, span)).astype(F32) == ids[pl.ds(3 * k, 1), :], 1.0, 0.0).astype(BF16)
        g_high, g_low = halves(src_grad)
        src_part = dot(pick, g_high) + dot(pick, g_low)
        first = isinstance(k, int) and k == 0
        src_sum[...] = src_part if first else src_sum[...] + src_part
        dst_sum[...] = dst_part if first else dst_sum[...] + dst_part
        return carry

    if sets <= 2:
        for k in range(sets):
            one(k, 0)
    else:
        src_sum[...] = jnp.zeros(src_sum.shape, F32)
        dst_sum[...] = jnp.zeros(dst_sum.shape, F32)
        lax.fori_loop(0, sets, one, 0)


def first_grads_kernel(own, sets, place, *refs):
    pieces, swapped, q_ref, r_ref = refs[:sets], refs[sets : 2 * sets], refs[2 * sets], refs[2 * sets + 1]
    id_refs, (dst_ref, src_sum, dst_sum, ids) = refs[2 * sets + 2 : 3 * sets + 2], refs[3 * sets + 2 :]
    assembled(place[0], own, pieces, swapped, dst_ref)
    add_grads(0, sets, dst_ref[...], q_ref, r_ref, reader(id_refs, own), ids, src_sum, dst_sum)


def last_grads_kernel(own, sets, place, table_ref, q_ref, r_ref, *refs):
    id_refs, (mine_ref, other_ref, ids, src_sum, dst_sum) = refs[:sets], refs[sets:]
    add_grads(1, sets, table_ref[...], q_ref, r_ref, reader(id_refs, own), ids, src_sum, dst_sum)
    partner = place[0] + 1 - 2 * lax.rem(place[0], 2)
    for who, out_ref in ((place[0], mine_ref), (partner, other_ref)):
        rows = pl.ds(pl.multiple_of(who * own, own), own)
        out_ref[:own, :] = src_sum[rows, :]
        out_ref[own:, :] = dst_sum[rows, :]


def step_kernel(width, mine_ref, other_ref, table_ref, out_ref):
    out_ref[...], _ = stepped(table_ref[...], mine_ref[...] + other_ref[...], width)


def finish_dst_kernel(width, mine_ref, other_ref, dst_ref, dst_out):
    dst_out[...], _ = stepped(dst_ref[...], mine_ref[...] + other_ref[...], width)


def finish_src_kernel(width, mine_ref, other_ref, src_ref, src_out, src_state_out):
    rows, state = stepped(src_ref[...], mine_ref[...] + other_ref[...], width)
    src_out[...] = narrowed(rows, width)
    src_state_out[...] = row_of(state)


def moved(value, dom, edge):
    groups, shards = lax.axis_size("dom"), lax.axis_size("edge")
    pairs = [
        (group * shards + place, (group + dom) % groups * shards + edge(place) % shards)
        for group in range(groups)
        for place in range(shards)
    ]
    return lax.ppermute(value, ("dom", "edge"), pairs)


def call(kernel, name, out_shape, in_specs, out_specs, scratch=(), prefetch=0, grid=(1,), flops=0, moved=0, vmem=24):
    return pl.pallas_call(
        kernel,
        out_shape=out_shape,
        grid_spec=pltpu.PrefetchScalarGridSpec(
            num_scalar_prefetch=prefetch,
            grid=grid,
            in_specs=in_specs,
            out_specs=out_specs,
            scratch_shapes=list(scratch),
        ),
        compiler_params=pltpu.CompilerParams(vmem_limit_bytes=int(vmem * 2**20)),
        cost_estimate=pl.CostEstimate(flops=flops, bytes_accessed=moved, transcendentals=0),
        name=name,
    )


def block(shape, at=None):
    at = (0,) * len(shape) if at is None else at
    return pl.BlockSpec(shape, lambda *_: at)


def on_device(
    src_table, src_state, dst_table, dst_state, relations, edge_src, edge_rel, edge_dst, negatives
):
    width = src_table.shape[1]
    own = src_table.shape[0]
    shards = lax.axis_size("edge")
    sets = shards // 2
    entities = own * shards
    edges = edge_src.shape[1]
    span = round_up(edges, LANES)
    half, padded = half_lanes(width)
    wide = 2 * padded
    tiles = wide // LANES
    assert shards % 2 == 0 and half % 8 == 0 and own % 8 == 0 and span == wide
    assert negatives.shape[1] == 1 and negatives.shape[2] <= span

    def rows(count):
        return jax.ShapeDtypeStruct((count, wide), F32)

    own_block = block((own, wide))
    src_block = block((own + 8, wide))
    table_block = block((entities, wide))
    q_block = block((sets * span, wide))

    def rel_block(bucket):
        return block((sets * span * tiles, LANES), (bucket, 0))

    names = relations.shape[0]
    listed = (round_up(2 * sets * span // LANES, 8), LANES)
    rotate_scratch = [pltpu.VMEM((round_up(sets, 8), span), F32)]
    big = 24 if sets <= 2 else 48
    work = sets * span * wide
    grads_cost = dict(flops=2 * work * entities * 18, moved=work * 4 * 2, vmem=big)
    rotate_cost = dict(flops=2 * work * entities * 6, moved=work * 4 * 2, vmem=big)

    inputs = (
        src_table, src_state.reshape(1, own), dst_table, dst_state.reshape(1, own),
        edge_src, edge_rel, edge_dst, negatives,
    )
    src_own, dst_own = call(
        functools.partial(pack_kernel, width),
        "pack",
        (rows(own + 8), rows(own)),
        [pl.BlockSpec(memory_space=pltpu.HBM)] * 8,
        (src_block, own_block),
        [pltpu.VMEM(x.shape, x.dtype) for x in inputs]
        + [pltpu.VMEM((own, wide), F32), pltpu.SemaphoreType.DMA((8,))],
        vmem=24,
    )(*(pltpu.with_memory_space_constraint(x, pltpu.HBM) for x in inputs))

    dst_here = [moved(dst_own, 1, lambda e, k=k: e + 2 * k) for k in range(sets)]
    src_here = [src_own] + [moved(src_own, 0, lambda e, k=k: e + 2 * k) for k in range(1, sets)]

    def swapped(value):
        return moved(value, 0, lambda e: e ^ 1)

    src_there = [swapped(x) for x in src_here]
    place = lax.axis_index("edge").reshape(1).astype(jnp.int32)

    rel_shape = (2 * sets * span * tiles, LANES)
    rel_rows = call(
        functools.partial(relations_kernel, width, own, sets),
        "relations",
        jax.ShapeDtypeStruct(rel_shape, F32),
        [pl.BlockSpec(memory_space=pltpu.HBM)] + [src_block] * sets,
        block(rel_shape),
        [
            pltpu.VMEM((round_up(names, LANES) * tiles, LANES), F32),
            pltpu.VMEM((width, names), F32),
            pltpu.VMEM(listed, jnp.int32),
            pltpu.SMEM(listed, jnp.int32),
            pltpu.SemaphoreType.DMA((tiles,)),
            pltpu.SemaphoreType.DMA(()),
        ],
        moved=names * width * 4,
        flops=names * width * 2048,
        vmem=46,
    )(relations.T, *src_here)

    rel_rows, dst_here = lax.optimization_barrier((rel_rows, dst_here))
    dst_there = [swapped(x) for x in dst_here]

    src_whole, turned = call(
        functools.partial(first_rotate_kernel, own, sets),
        "rotate0",
        (rows(entities), rows(sets * span)),
        [src_block] * (2 * sets) + [rel_block(0)],
        (table_block, q_block),
        rotate_scratch,
        prefetch=1,
        **rotate_cost,
    )(place, *src_here, *src_there, rel_rows)

    id_scratch = pltpu.VMEM((round_up(3 * sets, 8), span), F32)
    dst_whole, src_mine, dst_mine = call(
        functools.partial(first_grads_kernel, own, sets),
        "grads0",
        (rows(entities),) * 3,
        [own_block] * (2 * sets) + [q_block, rel_block(0)] + [src_block] * sets,
        (table_block,) * 3,
        [id_scratch],
        prefetch=1,
        **grads_cost,
    )(place, *dst_here, *dst_there, turned, rel_rows, *src_here)

    dst_other = swapped(dst_mine)
    src_other = swapped(src_mine)
    dst_whole = call(
        functools.partial(step_kernel, width),
        "step",
        rows(entities),
        [table_block] * 3,
        table_block,
    )(dst_mine, dst_other, dst_whole)
    dst_whole = moved(dst_whole, 1, lambda e: e)

    src_whole, turned = call(
        functools.partial(next_rotate_kernel, width, own, sets),
        "rotate1",
        (rows(entities), rows(sets * span)),
        [table_block] * 3 + [src_block] * sets + [rel_block(1)],
        (table_block, q_block),
        rotate_scratch,
        **rotate_cost,
    )(src_mine, src_other, src_whole, *src_here, rel_rows)

    both_block = block((2 * own, wide))
    mine, other = call(
        functools.partial(last_grads_kernel, own, sets),
        "grads1",
        (rows(2 * own),) * 2,
        [table_block, q_block, rel_block(1)] + [src_block] * sets,
        (both_block,) * 2,
        [id_scratch, pltpu.VMEM((entities, wide), F32), pltpu.VMEM((entities, wide), F32)],
        prefetch=1,
        **grads_cost,
    )(place, dst_whole, turned, rel_rows, *src_here)

    other = swapped(other)
    part_block = pl.BlockSpec((own, wide), lambda i, place: (place[0], 0))

    def half_block(at):
        return pl.BlockSpec((own, wide), lambda i, place: (at, 0))

    dst_rows = call(
        lambda place_ref, *refs: finish_dst_kernel(width, *refs),
        "finish_dst",
        rows(own),
        [half_block(1), half_block(1), part_block],
        own_block,
        prefetch=1,
    )(place, mine, other, dst_whole)
    dst_rows = moved(dst_rows, -2, lambda e: e)
    src_out, src_state_out = call(
        lambda place_ref, *refs: finish_src_kernel(width, *refs),
        "finish_src",
        (jax.ShapeDtypeStruct((own, width), F32), jax.ShapeDtypeStruct((1, own), F32)),
        [half_block(0), half_block(0), part_block],
        (block((own, width)), block((1, own))),
        prefetch=1,
        flops=10**8,
        moved=10**6,
    )(place, mine, other, src_whole)
    dst_out, dst_state_out = call(
        functools.partial(unpack_kernel, width),
        "unpack",
        (jax.ShapeDtypeStruct((own, width), F32), jax.ShapeDtypeStruct((1, own), F32)),
        [own_block],
        (block((own, width)), block((1, own))),
    )(dst_rows)
    return src_out, src_state_out.reshape(own), dst_out, dst_state_out.reshape(own)


def solution(mesh):
    return jax.shard_map(
        on_device,
        mesh=mesh,
        in_specs=(
            P(("dom", "edge"), None),
            P(("dom", "edge")),
            P(("dom", "edge"), None),
            P(("dom", "edge")),
            P(),
            P(None, ("dom", "edge")),
            P(None, ("dom", "edge")),
            P(None, ("dom", "edge")),
            P(None, ("dom", "edge"), None),
        ),
        out_specs=(
            P(("dom", "edge"), None),
            P(("dom", "edge")),
            P(("dom", "edge"), None),
            P(("dom", "edge")),
        ),
        check_vma=False,
    )
```
